32 devices in a mesh: groups: 2 (over x), ctx: 16 (over z, y, core).
Axes of the slice: x: 2, y: 2, z: 4, core: 2. Of those that a mesh axis runs over, the one named last changes fastest.
Arguments:
- queries: bfloat16 [12288, 1024], P(('groups', 'ctx')), parts along dimension 0
- keys: bfloat16 [12288, 1024], P(('groups', 'ctx')), parts along dimension 0
- values: bfloat16 [12288, 1024], P(('groups', 'ctx')), parts along dimension 0, may hold values from -6 to 6
- out_weight: bfloat16 [1024, 1024], P('ctx'), may hold values from -0.1875 to 0.1875
- grad_output: bfloat16 [12288, 1024], P(('groups', 'ctx')), parts along dimension 0, may hold values from -6 to 6
- complex_id: int32 [12288], P('groups'), parts along dimension 0, may hold values from 0 to 3, never falling along the last dimension, each value on 1 to 3072 neighbouring positions
- contacts: int32 [96, 6], P(('groups', 'ctx')), parts along dimension 0, may hold values from 0 to 47, as said below
- contact_count: int32 [96], P(('groups', 'ctx')), parts along dimension 0, may hold values from 3 to 6, as said below
Outputs:
- mixed: bfloat16 [12288, 1024], P(('groups', 'ctx')), parts along dimension 0
- grad_queries: bfloat16 [12288, 1024], P(('groups', 'ctx')), parts along dimension 0
- grad_keys: bfloat16 [12288, 1024], P(('groups', 'ctx')), parts along dimension 0
- grad_values: bfloat16 [12288, 1024], P(('groups', 'ctx')), parts along dimension 0
- grad_weight: float32 [2048, 1024], P(('groups', 'ctx')), parts along dimension 0
The draws below stay inside these ranges and needn't reach their ends.
There are 2 independent parts, one for each index of `groups`. The reference program is written for one: setup_inputs(seed, part) draws one part's arguments, and reference() takes and returns one part's arrays. A program takes and returns all parts, laid end to end along the dimension named above; an argument that names none is the same for every part. Nothing has to cross between parts.
Inputs may be any that keep to these rules, and one draw needn't show every extreme that they name: `contacts`: entry 0 of each list is the query block itself; the other entries are distinct blocks, other than the query block, at most 6 blocks from it. `contact_count`: on some device every block of the device has all 6 entries live.
All inputs are finite; a program needn't handle non-finite values.
Results may differ from the reference program's by a relative error of at most 0.022.
Values may be sent and summed in bfloat16 or wider, within the bound.
A program may use at most 192 MiB of HBM per device.

```python
import math
import jax
import jax.numpy as jnp
import numpy as np
from jax import lax

HEADS = 16
D = 1024
BLOCKS_DEV = 3
LISTED = 6
TOK_DEV = 384
TOKENS = 6144
AMINO_TILE_COUNT = 48
NEIGHBOR_RADIUS = 6
N_CTX = 16


def query_key_pair(key):
    key_query = jax.random.fold_in(key, 101)
    key_keys = jax.random.fold_in(key, 202)
    queries_out = jax.random.normal(key_query, (TOKENS, D), jnp.float32)
    keys_out = jax.random.normal(key_keys, (TOKENS, D), jnp.float32)
    return (queries_out, keys_out)


def draw_queries(key, part):
    return query_key_pair(key)[0].astype(jnp.bfloat16)


def draw_keys(key, part):
    return query_key_pair(key)[1].astype(jnp.bfloat16)


def draw_contacts(key, part):
    generator_state = jax.random.fold_in(key, 11)
    key_up = jax.random.fold_in(key, 12)
    key_down = jax.random.fold_in(key, 13)
    blocks = jnp.arange(AMINO_TILE_COUNT, dtype=jnp.int32)
    offsets = jnp.concatenate([jnp.arange(-NEIGHBOR_RADIUS, 0, dtype=jnp.int32), jnp.arange(1, NEIGHBOR_RADIUS + 1, dtype=jnp.int32)])
    target = blocks[:, None] + offsets[None, :]
    inside = (target >= 0) & (target < AMINO_TILE_COUNT)
    partner_tile_index = jnp.arange(2 * NEIGHBOR_RADIUS, dtype=jnp.int32)[None, :]
    higher_partner_pick = NEIGHBOR_RADIUS + jax.random.randint(key_up, (AMINO_TILE_COUNT, 1), 0, NEIGHBOR_RADIUS)
    lower_partner_pick = jax.random.randint(key_down, (AMINO_TILE_COUNT, 1), 0, NEIGHBOR_RADIUS)
    logit_increment = jnp.where(partner_tile_index == higher_partner_pick, 1 << 27, 0) + jnp.where(partner_tile_index == lower_partner_pick, 1 << 26, 0)
    similarity_logits = jax.random.randint(generator_state, (AMINO_TILE_COUNT, 2 * NEIGHBOR_RADIUS), 0, 1 << 20) * (2 * NEIGHBOR_RADIUS) + partner_tile_index + logit_increment
    similarity_logits = jnp.where(inside, similarity_logits, -1 - partner_tile_index)
    chosen = lax.top_k(similarity_logits, LISTED - 1)[1]
    picked = jnp.take_along_axis(target, chosen, axis=1)
    return jnp.concatenate([blocks[:, None], picked], axis=1).astype(jnp.int32)


def draw_contact_count(key, part):
    devices = AMINO_TILE_COUNT // BLOCKS_DEV
    key_heavy = jax.random.fold_in(key, 7)
    key_forced = jax.random.fold_in(key, 8)
    key_light = jax.random.fold_in(key, 9)
    heavy = jax.random.randint(key_heavy, (devices,), 0, 4) == 0
    forced = jax.random.randint(key_forced, (), 0, devices)
    heavy = heavy | (jnp.arange(devices, dtype=jnp.int32) == forced)
    low = min(3, LISTED)
    light = jax.random.randint(key_light, (AMINO_TILE_COUNT,), low, max(low, LISTED // 2 + 1) + 1)
    heavy_rows = jnp.repeat(heavy, BLOCKS_DEV)
    return jnp.where(heavy_rows, LISTED, light).astype(jnp.int32)


def levels(stream_key, shape, cuts, least, top_value):
    def one(dim, blocks):
        steps = jax.random.uniform(jax.random.fold_in(jax.random.fold_in(stream_key, 6), dim), (blocks,), jnp.float32, least / len(cuts), top_value / len(cuts))
        return jnp.repeat(jnp.exp(steps), shape[dim] // blocks).reshape((-1,) + (1,) * (len(shape) - dim - 1))

    factor_of = one(*cuts[0])
    for cut in cuts[1:]:
        factor_of = factor_of * one(*cut)
    return factor_of


def split_up(number_of, total, reach, skew):
    loads = [(1 << 20) // math.isqrt(grade ** skew) + 1 for grade in range(2, number_of + 1)]
    surplus, counts = total - reach - (number_of - 1), [1] * (number_of - 1)
    while surplus > 0:
        candidates = [i for i in range(number_of - 1) if counts[i] < reach]
        pool, remaining = sum([loads[i] for i in candidates]), surplus
        for i in candidates:
            more = min(reach - counts[i], max(1, remaining * loads[i] // pool), surplus)
            counts[i] = counts[i] + more
            surplus = surplus - more
    return np.array([reach] + counts)


def uneven(own_key, count, total, reach, lean):
    if count == 2:
        one = jax.random.randint(own_key, (), max(1, total - reach), min(reach, total - 1) + 1)
        return jnp.stack([one, total - one])
    sizes = jnp.asarray(split_up(count, total, reach, lean), jnp.int32)
    twos = (count - 1) // 2
    giver, receiver = sizes[1:1 + 2 * twos:2], sizes[2:2 + 2 * twos:2]
    margin = jnp.minimum(giver - 1, reach - receiver)
    moved = jax.random.randint(jax.random.fold_in(own_key, 1), (twos,), 0, 1 << 20) % (margin + 1)
    sizes = sizes.at[1:1 + 2 * twos:2].set(giver - moved).at[2:2 + 2 * twos:2].set(receiver + moved)
    return sizes[jax.random.permutation(jax.random.fold_in(own_key, 2), count)]


def bell_draw(rng, extent, spread, reach, shards=(), held_as=jnp.bfloat16):
    drawn = spread * jax.random.normal(rng, extent, jnp.float32)
    if shards:
        drawn = drawn * levels(rng, extent, shards, -0.22, 0.18)
    return jnp.clip(drawn, -reach, reach).astype(held_as)


def setup_inputs(seed: int = 0, part: int = 0) -> dict:
    key_list = jax.random.split(jax.random.key(seed), 9)
    part_splits = jax.random.split(jax.random.fold_in(key_list[8], part), 9)
    return {
        "queries": draw_queries(jax.random.fold_in(jax.random.fold_in(key_list[8], part), 71), part),
        "keys": draw_keys(jax.random.fold_in(jax.random.fold_in(key_list[8], part), 71), part),
        "values": bell_draw(part_splits[2], (TOKENS, D), 1.0, 6.0, ((0, 16),)),
        "out_weight": bell_draw(key_list[3], (D, D), D ** -0.5, 0.1875, ((0, 16),)),
        "grad_output": bell_draw(part_splits[4], (TOKENS, D), 1.0, 6.0, ((0, 16),)),
        "complex_id": jnp.searchsorted(jnp.cumsum(uneven(part_splits[5], N_CTX // 4, TOKENS, 8 * TOK_DEV, 0)), jnp.arange(TOKENS), side="right").astype(jnp.int32),
        "contacts": draw_contacts(jax.random.fold_in(jax.random.fold_in(key_list[8], part), 71), part),
        "contact_count": draw_contact_count(jax.random.fold_in(jax.random.fold_in(key_list[8], part), 71), part),
    }


def block_pass(query, block_keys, block_values, grad_block, allowed):
    rows, width = query.shape
    head_dim = width // HEADS
    scale = 1.0 / math.sqrt(head_dim)
    query_heads = query.astype(jnp.float32).reshape(rows, HEADS, head_dim)
    key_heads = block_keys.astype(jnp.float32).reshape(-1, HEADS, head_dim)
    value_heads = block_values.astype(jnp.float32).reshape(-1, HEADS, head_dim)
    grad_heads = grad_block.astype(jnp.float32).reshape(rows, HEADS, head_dim)
    similarity_logits = jnp.einsum('qhd,khd->hqk', query_heads, key_heads) * scale
    masked = jnp.where(allowed[None], similarity_logits, jnp.float32(-1e+30))
    top = lax.optimization_barrier(jnp.max(masked, axis=2, keepdims=True))
    total = lax.optimization_barrier(jnp.sum(jnp.where(allowed[None], jnp.exp(masked - top), jnp.float32(0.0)), axis=2, keepdims=True))
    log_total = top + jnp.log(total)
    probs = jnp.where(allowed[None], jnp.exp(masked - log_total), jnp.float32(0.0))
    probs_low = lax.optimization_barrier(probs.astype(jnp.bfloat16)).astype(jnp.float32)
    attended = jnp.einsum('hqk,khd->qhd', probs_low, value_heads).astype(jnp.bfloat16)
    attended_wide = lax.optimization_barrier(attended).astype(jnp.float32)
    row_dot = jnp.einsum('qhd,qhd->hq', grad_heads, attended_wide)[..., None]
    grad_probs = jnp.einsum('qhd,khd->hqk', grad_heads, value_heads)
    grad_scores = lax.optimization_barrier((probs * (grad_probs - row_dot)).astype(jnp.bfloat16)).astype(jnp.float32)
    grad_query = (jnp.einsum('hqk,khd->qhd', grad_scores, key_heads) * scale).reshape(rows, width)
    grad_key = (jnp.einsum('hqk,qhd->khd', grad_scores, query_heads) * scale).reshape(-1, width)
    grad_value = jnp.einsum('hqk,qhd->khd', probs_low, grad_heads).reshape(-1, width)
    return (attended.reshape(rows, width), grad_query.astype(jnp.bfloat16), grad_key, grad_value)

def reference(queries, keys, values, out_weight, grad_output, complex_id, contacts, contact_count):
    tokens, width = queries.shape
    nblocks, listed = contacts.shape
    block = tokens // nblocks
    grad_input = jnp.dot(grad_output, out_weight.T, preferred_element_type=jnp.float32).astype(jnp.bfloat16)
    query_blocks = queries.reshape(nblocks, block, width)
    key_blocks = keys.reshape(nblocks, block, width)
    value_blocks = values.reshape(nblocks, block, width)
    grad_blocks = grad_input.reshape(nblocks, block, width)
    id_blocks = complex_id.reshape(nblocks, block)
    slot_live = jnp.arange(listed, dtype=jnp.int32)[None, :] < contact_count[:, None]

    def step(carry, index):
        key_grads, value_grads = carry
        chosen = contacts[index]
        gathered_keys = key_blocks[chosen].reshape(listed * block, width)
        gathered_values = value_blocks[chosen].reshape(listed * block, width)
        live = jnp.repeat(slot_live[index], block)
        allowed = (id_blocks[index][:, None] == id_blocks[chosen].reshape(-1)[None, :]) & live[None, :]
        attended, grad_query, grad_key, grad_value = block_pass(query_blocks[index], gathered_keys, gathered_values, grad_blocks[index], allowed)
        key_grads = key_grads.at[chosen].add(grad_key.reshape(listed, block, width))
        value_grads = value_grads.at[chosen].add(grad_value.reshape(listed, block, width))
        return ((key_grads, value_grads), (attended, grad_query))
    start = jnp.zeros((nblocks, block, width), jnp.float32)
    (key_grads, value_grads), (attended, grad_query) = lax.scan(step, (start, start), jnp.arange(nblocks, dtype=jnp.int32))
    attended = attended.reshape(tokens, width)
    mixed = jnp.dot(attended, out_weight, preferred_element_type=jnp.float32).astype(jnp.bfloat16)
    grad_weight = jnp.dot(attended.T, grad_output, preferred_element_type=jnp.float32) * jnp.float32(1.0 / math.sqrt(tokens))
    return (mixed, grad_query.reshape(tokens, width), key_grads.reshape(tokens, width).astype(jnp.bfloat16), value_grads.reshape(tokens, width).astype(jnp.bfloat16), grad_weight)
```

```python
import functools
import math

import jax
import jax.numpy as jnp
from jax import lax
from jax.experimental import pallas as pl
from jax.experimental.pallas import tpu as pltpu
from jax.sharding import PartitionSpec as P

HEADS = 16
REACH_DEV = 2
LANES = 128


def shift(array, axis, by):
    length = lax.axis_size(axis)
    pairs = [(i, i + by) for i in range(length) if 0 <= i + by < length]
    return lax.ppermute(array, axis, pairs)


def attention_kernel(
    blocks, listed, block, head_dim,
    local_ref, count_ref, q_ref, k_ref, v_ref, d_ref,
    below2, below1, above1, above2, idk_ref, idq_ref,
    att_ref, dq_ref, own_ref, far_ref,
    kwin, vwin, bias, gk, gv, kg, vg,
):
    rows = blocks * block
    scale = 1.0 / math.sqrt(head_dim)
    f32, bf16 = jnp.float32, jnp.bfloat16

    @pl.when(pl.program_id(0) == 0)
    def _():
        for b in range(blocks):
            mine = idq_ref[b : b + 1, :]
            for j in range(listed):
                start = pl.multiple_of(local_ref[b, j] * block, block)
                same = idk_ref[pl.ds(start, block), :] == mine
                alive = jnp.where(j < count_ref[b], 0.0, -jnp.inf).astype(f32)
                bias[pl.ds((b * listed + j) * block, block), :] = jnp.where(same, alive, -jnp.inf)

    for i, piece in enumerate((below2, below1, None, above1, above2)):
        span = pl.ds(i * rows, rows)
        kwin[span, :] = k_ref[...] if piece is None else piece[0]
        vwin[span, :] = v_ref[...] if piece is None else piece[1]
    gk[...] = jnp.zeros_like(gk)
    gv[...] = jnp.zeros_like(gv)

    lane = lax.broadcasted_iota(jnp.int32, (block, LANES), 1) < head_dim
    sub = lax.broadcasted_iota(jnp.int32, (LANES, block), 0) < head_dim
    last = (((1,), (1,)), ((), ()))
    first = (((0,), (0,)), ((), ()))

    def two(x):
        zero = jnp.zeros_like(x)
        return jnp.concatenate([jnp.where(lane, x, zero), jnp.where(lane, zero, x)], axis=0).astype(bf16)

    for b in range(blocks):
        here = pl.ds(b * block, block)
        starts = [pl.multiple_of(local_ref[b, j] * block, block) for j in range(listed)]
        for j in range(listed):
            kg[pl.ds(j * block, block), :] = kwin[pl.ds(starts[j], block), :]
            vg[pl.ds(j * block, block), :] = vwin[pl.ds(starts[j], block), :]
        grad = d_ref[here, :].astype(f32)
        q2 = two(q_ref[here, :].astype(f32) * scale)
        d2 = two(grad)
        s = lax.dot_general(kg[...], q2, last, preferred_element_type=f32)
        mask = bias[pl.ds(b * listed * block, listed * block), :]
        s = s + jnp.concatenate([mask, mask], axis=1)
        top = jnp.max(s, axis=0, keepdims=True)
        e = jnp.exp(s - top)
        probs = e * (1.0 / jnp.sum(e, axis=0, keepdims=True))
        low = probs.astype(bf16)
        ot = lax.dot_general(vg[...], low, first, preferred_element_type=f32)
        att = jnp.where(sub, ot[:, :block], ot[:, block:]).astype(bf16).astype(f32)
        att_ref[here, :] = att.T.astype(bf16)
        prod = grad.T * att
        row_dot = jnp.concatenate(
            [jnp.sum(prod[:head_dim], axis=0, keepdims=True), jnp.sum(prod[head_dim:], axis=0, keepdims=True)],
            axis=1,
        )
        dp = lax.dot_general(vg[...], d2, last, preferred_element_type=f32)
        ds = (probs * (dp - row_dot)).astype(bf16)
        dqt = lax.dot_general(kg[...], ds, first, preferred_element_type=f32)
        dq = jnp.where(sub, dqt[:, :block], dqt[:, block:]) * scale
        dq_ref[here, :] = dq.T.astype(bf16)
        dk = jnp.dot(ds, q2, preferred_element_type=f32)
        dv = jnp.dot(low, d2, preferred_element_type=f32)
        for j in range(listed):
            part = slice(j * block, (j + 1) * block)
            gk[pl.ds(starts[j], block), :] += dk[part]
            gv[pl.ds(starts[j], block), :] += dv[part]

    own = pl.ds(REACH_DEV * rows, rows)
    own_ref[0] = gk[own, :]
    own_ref[1] = gv[own, :]
    for i, at in enumerate((0, 1, 3, 4)):
        span = pl.ds(at * rows, rows)
        far_ref[i, 0] = gk[span, :].astype(bf16)
        far_ref[i, 1] = gv[span, :].astype(bf16)


def attention(local, count, queries, keys, values, grad_input, pieces, idk, idq):
    rows, width = queries.shape
    blocks, listed = local.shape
    block = rows // blocks
    head_dim = width // HEADS
    window = (2 * REACH_DEV + 1) * rows
    flat = pl.BlockSpec((rows, LANES), lambda p, *_: (0, p))
    pair = pl.BlockSpec((2, rows, LANES), lambda p, *_: (0, 0, p))
    far = pl.BlockSpec((2 * REACH_DEV, 2, rows, LANES), lambda p, *_: (0, 0, 0, p))
    whole = lambda shape: pl.BlockSpec(shape, lambda p, *_: (0, 0))
    f32, bf16 = jnp.float32, jnp.bfloat16
    return pl.pallas_call(
        functools.partial(attention_kernel, blocks, listed, block, head_dim),
        grid_spec=pltpu.PrefetchScalarGridSpec(
            num_scalar_prefetch=2,
            grid=(width // LANES,),
            in_specs=[flat, flat, flat, flat, pair, pair, pair, pair, whole(idk.shape), whole(idq.shape)],
            out_specs=[flat, flat, pair, far],
            scratch_shapes=[
                pltpu.VMEM((window, LANES), bf16),
                pltpu.VMEM((window, LANES), bf16),
                pltpu.VMEM((blocks * listed * block, LANES), f32),
                pltpu.VMEM((window, LANES), f32),
                pltpu.VMEM((window, LANES), f32),
                pltpu.VMEM((listed * block, LANES), bf16),
                pltpu.VMEM((listed * block, LANES), bf16),
            ],
        ),
        out_shape=[
            jax.ShapeDtypeStruct((rows, width), bf16),
            jax.ShapeDtypeStruct((rows, width), bf16),
            jax.ShapeDtypeStruct((2, rows, width), f32),
            jax.ShapeDtypeStruct((2 * REACH_DEV, 2, rows, width), bf16),
        ],
        compiler_params=pltpu.CompilerParams(dimension_semantics=("arbitrary",)),
        name="contact_attention",
    )(local, count, queries, keys, values, grad_input, *pieces, idk, idq)


def shards(queries, keys, values, out_weight, grad_output, complex_id, contacts, contact_count):
    rows, width = queries.shape
    local_blocks, listed = contacts.shape
    block = rows // local_blocks
    position = lax.axis_index("ctx")
    total_tokens = rows * lax.axis_size("ctx")
    f32, bf16 = jnp.float32, jnp.bfloat16
    weight = lax.all_gather(out_weight, "ctx", axis=0, tiled=True)
    pair = jnp.stack([keys, values])
    below1 = shift(pair, "ctx", 1)
    above1 = shift(pair, "ctx", -1)
    below2 = shift(below1, "ctx", 1)
    above2 = shift(above1, "ctx", -1)
    grad_input = lax.dot_general(
        grad_output, weight, (((1,), (1,)), ((), ())), preferred_element_type=f32
    ).astype(bf16)
    margin = REACH_DEV * rows
    ids = lax.dynamic_slice_in_dim(
        jnp.pad(complex_id, (margin, margin), constant_values=-1), position * rows, rows + 2 * margin
    )
    idk = jnp.broadcast_to(ids[:, None], (rows + 2 * margin, LANES))
    idq = ids[margin : margin + rows].reshape(local_blocks, block)
    local = contacts - (position - REACH_DEV) * local_blocks
    attended, grad_queries, own, far = attention(
        local, contact_count, queries, keys, values, grad_input,
        (below2, below1, above1, above2), idk, idq,
    )
    upward = shift(far[3], "ctx", 1)
    downward = shift(far[0], "ctx", -1)
    upward = shift((upward.astype(f32) + far[2].astype(f32)).astype(bf16), "ctx", 1)
    downward = shift((downward.astype(f32) + far[1].astype(f32)).astype(bf16), "ctx", -1)
    grads = (own + upward.astype(f32) + downward.astype(f32)).astype(bf16)
    mixed = jnp.dot(attended, weight, preferred_element_type=f32).astype(bf16)
    grad_weight = lax.psum_scatter(
        lax.dot_general(attended, grad_output, (((0,), (0,)), ((), ())), preferred_element_type=f32),
        "ctx",
        scatter_dimension=0,
        tiled=True,
    ) * jnp.float32(1.0 / math.sqrt(total_tokens))
    return mixed, grad_queries, grads[0], grads[1], grad_weight


def solution(mesh):
    split = P(("groups", "ctx"), None)
    return jax.shard_map(
        shards,
        mesh=mesh,
        in_specs=(split, split, split, P("ctx", None), split, P("groups"), split, P(("groups", "ctx"))),
        out_specs=(split,) * 5,
        check_vma=False,
    )
```

```python
import functools
import math

import jax
import jax.numpy as jnp
from jax import lax
from jax.experimental import pallas as pl
from jax.experimental.pallas import tpu as pltpu
from jax.sharding import PartitionSpec as P

HEADS = 16
REACH_DEV = 2
LANES = 128


def neighbours(n):
    me = lax.axis_index("ctx")
    core, y = lax.rem(me, 2), lax.rem(me // 2, 2)
    ahead, behind = me + 4 - 8 * y, me - 4 + 8 * y
    has_ahead = (ahead >= 0) & (ahead < n)
    has_behind = (behind >= 0) & (behind < n)
    return core, y, me + 2 - 4 * y, me + 1 - 2 * core, ahead, behind, has_ahead, has_behind


def greet(ypeer, cpeer, ahead, behind, has_ahead, has_behind):
    barrier = pltpu.get_barrier_semaphore()

    def hello(device):
        pl.semaphore_signal(barrier, inc=1, device_id={"ctx": device}, device_id_type=pl.DeviceIdType.MESH)

    hello(ypeer)
    hello(cpeer)
    pl.when(has_ahead)(lambda: hello(ahead))
    pl.when(has_behind)(lambda: hello(behind))
    pl.semaphore_wait(barrier, 2 + has_ahead.astype(jnp.int32) + has_behind.astype(jnp.int32))


def remote(src, dst, send, recv, device):
    return pltpu.make_async_remote_copy(
        src_ref=src, dst_ref=dst, send_sem=send, recv_sem=recv,
        device_id={"ctx": device}, device_id_type=pl.DeviceIdType.MESH,
    )


def gather_kernel(n, chunks, k_ref, v_ref, kwin, vwin, sends, recvs):
    core, y, ypeer, cpeer, ahead, behind, has_ahead, has_behind = neighbours(n)
    greet(ypeer, cpeer, ahead, behind, has_ahead, has_behind)
    step = k_ref.shape[0] // chunks
    owns, wins = (k_ref, v_ref), (kwin, vwin)
    total = 2 * chunks

    def at(c):
        return c % 2, pl.ds((c // 2) * step, step)

    def over_y(c):
        a, r = at(c)
        return remote(owns[a].at[r], wins[a].at[3 * y, r], sends.at[0, c], recvs.at[0, c], ypeer)

    def over_z(c):
        a, r = at(c)
        return remote(wins[a].at[3 - 3 * y, r], wins[a].at[3 * y, r], sends.at[1, c], recvs.at[1, c], ahead)

    def across(c):
        a, r = at(c)
        return remote(owns[a].at[r], wins[a].at[1 + core, r], sends.at[2, c], recvs.at[2, c], cpeer)

    def onward(c):
        a, r = at(c)
        return remote(
            wins[a].at[3 - 3 * core, r], wins[a].at[2 - core, r], sends.at[3, c], recvs.at[3, c], cpeer
        )

    def late(c):
        pl.when(has_behind)(lambda: over_z(c).wait_recv())
        pl.when(has_behind & (y != core))(lambda: onward(c).start())

    for c in range(total):
        over_y(c).start()
    for c in range(total):
        across(c).start()
    for c in range(total):
        over_y(c).wait_recv()
        pl.when(has_ahead)(lambda c=c: over_z(c).start())
        pl.when(y == core)(lambda c=c: onward(c).start())
        if c:
            late(c - 1)
    late(total - 1)
    for c in range(total):
        over_y(c).wait_send()
        pl.when(has_ahead)(lambda c=c: over_z(c).wait_send())
        across(c).wait_send()
        across(c).wait_recv()
        pl.when((y == core) | has_behind)(lambda c=c: onward(c).wait_send())
        pl.when((y != core) | has_behind)(lambda c=c: onward(c).wait_recv())


def gather_window(keys, values, chunks=6):
    n = lax.axis_size("ctx")
    any_space = pl.BlockSpec(memory_space=pl.ANY)
    shape = jax.ShapeDtypeStruct((2 * REACH_DEV,) + keys.shape, keys.dtype)
    return pl.pallas_call(
        functools.partial(gather_kernel, n, chunks),
        out_shape=[shape, shape],
        in_specs=[any_space] * 2,
        out_specs=[any_space] * 2,
        scratch_shapes=[pltpu.SemaphoreType.DMA((4, 2 * chunks)), pltpu.SemaphoreType.DMA((4, 2 * chunks))],
        compiler_params=pltpu.CompilerParams(collective_id=0, has_side_effects=True),
        cost_estimate=pl.CostEstimate(flops=0, bytes_accessed=150_000_000, transcendentals=0),
        name="gather_window",
    )(keys, values)


def return_kernel(n, chunks, far, own, gk_ref, gv_ref, got_f, got_c, got_z, got_y, put_z, put_y, sends, recvs):
    core, y, ypeer, cpeer, ahead, behind, has_ahead, has_behind = neighbours(n)
    greet(ypeer, cpeer, ahead, behind, has_ahead, has_behind)
    step = own.shape[1] // chunks
    total = 2 * chunks
    f32, bf16 = jnp.float32, jnp.bfloat16

    def at(c):
        return c % 2, pl.ds((c // 2) * step, step)

    def back(c):
        a, r = at(c)
        return remote(far.at[1 + core, a, r], got_f.at[a, r], sends.at[0, c], recvs.at[0, c], cpeer)

    def across(c):
        a, r = at(c)
        return remote(far.at[2 - core, a, r], got_c.at[a, r], sends.at[1, c], recvs.at[1, c], cpeer)

    def over_z(c):
        a, r = at(c)
        return remote(put_z.at[a, r], got_z.at[a, r], sends.at[2, c], recvs.at[2, c], behind)

    def over_y(c):
        a, r = at(c)
        return remote(put_y.at[a, r], got_y.at[a, r], sends.at[3, c], recvs.at[3, c], ypeer)

    sent_back = (y != core) | has_behind
    got_back = (y == core) | has_behind
    for c in range(total):
        pl.when(sent_back)(lambda c=c: back(c).start())

    def second(c):
        a, r = at(c)
        pl.when(has_ahead)(lambda: over_z(c).wait_recv())
        value = far[3 - 3 * y, a, r, :].astype(f32)
        value = value + jnp.where(has_ahead, got_z[a, r, :].astype(f32), 0.0)
        value = value + jnp.where(y == core, got_f[a, r, :].astype(f32), 0.0)
        put_y[a, r, :] = value.astype(bf16)
        over_y(c).start()

    for c in range(total):
        a, r = at(c)
        pl.when(got_back)(lambda c=c: back(c).wait_recv())
        value = far[3 * y, a, r, :].astype(f32)
        put_z[a, r, :] = (value + jnp.where(y != core, got_f[a, r, :].astype(f32), 0.0)).astype(bf16)
        pl.when(has_behind)(lambda c=c: over_z(c).start())
        across(c).start()
        if c >= 2:
            second(c - 2)
    second(total - 2)
    second(total - 1)
    for c in range(total):
        a, r = at(c)
        across(c).wait_recv()
        over_y(c).wait_recv()
        value = own[a, r, :] + got_c[a, r, :].astype(f32) + got_y[a, r, :].astype(f32)
        (gk_ref, gv_ref)[a][r, :] = value.astype(bf16)
    for c in range(total):
        pl.when(sent_back)(lambda c=c: back(c).wait_send())
        across(c).wait_send()
        pl.when(has_behind)(lambda c=c: over_z(c).wait_send())
        over_y(c).wait_send()


def return_grads(far, own, chunks=6):
    n = lax.axis_size("ctx")
    _, rows, width = own.shape
    space = pl.BlockSpec(memory_space=pltpu.VMEM)
    shape = jax.ShapeDtypeStruct((rows, width), jnp.bfloat16)
    return pl.pallas_call(
        functools.partial(return_kernel, n, chunks),
        out_shape=[shape, shape],
        in_specs=[space] * 2,
        out_specs=[space] * 2,
        scratch_shapes=[pltpu.VMEM((2, rows, width), jnp.bfloat16)] * 6
        + [pltpu.SemaphoreType.DMA((4, 2 * chunks)), pltpu.SemaphoreType.DMA((4, 2 * chunks))],
        compiler_params=pltpu.CompilerParams(
            collective_id=1, has_side_effects=True, vmem_limit_bytes=56 * 1024 * 1024
        ),
        cost_estimate=pl.CostEstimate(flops=0, bytes_accessed=150_000_000, transcendentals=0),
        name="return_grads",
    )(far, own)


def attention_kernel(
    blocks, listed, block, head_dim,
    local_ref, count_ref, q_ref, k_ref, v_ref, d_ref,
    kfar, vfar, idk_ref, idq_ref,
    att_ref, dq_ref, own_ref, far_ref,
    kwin, vwin, bias, gk, gv, kg, vg,
):
    rows = blocks * block
    scale = 1.0 / math.sqrt(head_dim)
    f32, bf16 = jnp.float32, jnp.bfloat16

    @pl.when(pl.program_id(0) == 0)
    def _():
        for b in range(blocks):
            mine = idq_ref[b : b + 1, :]
            for j in range(listed):
                start = pl.multiple_of(local_ref[b, j] * block, block)
                same = idk_ref[pl.ds(start, block), :] == mine
                alive = jnp.where(j < count_ref[b], 0.0, -jnp.inf).astype(f32)
                bias[pl.ds((b * listed + j) * block, block), :] = jnp.where(same, alive, -jnp.inf)

    for i, piece in enumerate((0, 1, None, 2, 3)):
        span = pl.ds(i * rows, rows)
        kwin[span, :] = k_ref[...] if piece is None else kfar[piece]
        vwin[span, :] = v_ref[...] if piece is None else vfar[piece]
    gk[...] = jnp.zeros_like(gk)
    gv[...] = jnp.zeros_like(gv)

    lane = lax.broadcasted_iota(jnp.int32, (block, LANES), 1) < head_dim
    sub = lax.broadcasted_iota(jnp.int32, (LANES, block), 0) < head_dim
    last = (((1,), (1,)), ((), ()))
    first = (((0,), (0,)), ((), ()))

    def two(x):
        zero = jnp.zeros_like(x)
        return jnp.concatenate([jnp.where(lane, x, zero), jnp.where(lane, zero, x)], axis=0).astype(bf16)

    for b in range(blocks):
        here = pl.ds(b * block, block)
        starts = [pl.multiple_of(local_ref[b, j] * block, block) for j in range(listed)]
        for j in range(listed):
            kg[pl.ds(j * block, block), :] = kwin[pl.ds(starts[j], block), :]
            vg[pl.ds(j * block, block), :] = vwin[pl.ds(starts[j], block), :]
        grad = d_ref[here, :].astype(f32)
        q2 = two(q_ref[here, :].astype(f32) * scale)
        d2 = two(grad)
        s = lax.dot_general(kg[...], q2, last, preferred_element_type=f32)
        mask = bias[pl.ds(b * listed * block, listed * block), :]
        s = s + jnp.concatenate([mask, mask], axis=1)
        top = jnp.max(s, axis=0, keepdims=True)
        e = jnp.exp(s - top)
        probs = e * (1.0 / jnp.sum(e, axis=0, keepdims=True))
        low = probs.astype(bf16)
        ot = lax.dot_general(vg[...], low, first, preferred_element_type=f32)
        att = jnp.where(sub, ot[:, :block], ot[:, block:]).astype(bf16).astype(f32)
        att_ref[here, :] = att.T.astype(bf16)
        prod = grad.T * att
        row_dot = jnp.concatenate(
            [jnp.sum(prod[:head_dim], axis=0, keepdims=True), jnp.sum(prod[head_dim:], axis=0, keepdims=True)],
            axis=1,
        )
        dp = lax.dot_general(vg[...], d2, last, preferred_element_type=f32)
        ds = (probs * (dp - row_dot)).astype(bf16)
        dqt = lax.dot_general(kg[...], ds, first, preferred_element_type=f32)
        dq = jnp.where(sub, dqt[:, :block], dqt[:, block:]) * scale
        dq_ref[here, :] = dq.T.astype(bf16)
        dk = jnp.dot(ds, q2, preferred_element_type=f32)
        dv = jnp.dot(low, d2, preferred_element_type=f32)
        for j in range(listed):
            part = slice(j * block, (j + 1) * block)
            gk[pl.ds(starts[j], block), :] += dk[part]
            gv[pl.ds(starts[j], block), :] += dv[part]

    own = pl.ds(REACH_DEV * rows, rows)
    own_ref[0] = gk[own, :]
    own_ref[1] = gv[own, :]
    for i, at in enumerate((0, 1, 3, 4)):
        span = pl.ds(at * rows, rows)
        far_ref[i, 0] = gk[span, :].astype(bf16)
        far_ref[i, 1] = gv[span, :].astype(bf16)


def attention(local, count, queries, keys, values, grad_input, kfar, vfar, idk, idq):
    rows, width = queries.shape
    blocks, listed = local.shape
    block = rows // blocks
    head_dim = width // HEADS
    window = (2 * REACH_DEV + 1) * rows
    flat = pl.BlockSpec((rows, LANES), lambda p, *_: (0, p))
    pair = pl.BlockSpec((2, rows, LANES), lambda p, *_: (0, 0, p))
    quad = pl.BlockSpec((2 * REACH_DEV, rows, LANES), lambda p, *_: (0, 0, p))
    far = pl.BlockSpec((2 * REACH_DEV, 2, rows, LANES), lambda p, *_: (0, 0, 0, p))
    whole = lambda shape: pl.BlockSpec(shape, lambda p, *_: (0, 0))
    f32, bf16 = jnp.float32, jnp.bfloat16
    return pl.pallas_call(
        functools.partial(attention_kernel, blocks, listed, block, head_dim),
        grid_spec=pltpu.PrefetchScalarGridSpec(
            num_scalar_prefetch=2,
            grid=(width // LANES,),
            in_specs=[flat, flat, flat, flat, quad, quad, whole(idk.shape), whole(idq.shape)],
            out_specs=[flat, flat, pair, far],
            scratch_shapes=[
                pltpu.VMEM((window, LANES), bf16),
                pltpu.VMEM((window, LANES), bf16),
                pltpu.VMEM((blocks * listed * block, LANES), f32),
                pltpu.VMEM((window, LANES), f32),
                pltpu.VMEM((window, LANES), f32),
                pltpu.VMEM((listed * block, LANES), bf16),
                pltpu.VMEM((listed * block, LANES), bf16),
            ],
        ),
        out_shape=[
            jax.ShapeDtypeStruct((rows, width), bf16),
            jax.ShapeDtypeStruct((rows, width), bf16),
            jax.ShapeDtypeStruct((2, rows, width), f32),
            jax.ShapeDtypeStruct((2 * REACH_DEV, 2, rows, width), bf16),
        ],
        compiler_params=pltpu.CompilerParams(dimension_semantics=("arbitrary",)),
        name="contact_attention",
    )(local, count, queries, keys, values, grad_input, kfar, vfar, idk, idq)


def shards(queries, keys, values, out_weight, grad_output, complex_id, contacts, contact_count):
    rows, width = queries.shape
    local_blocks, listed = contacts.shape
    block = rows // local_blocks
    position = lax.axis_index("ctx")
    total_tokens = rows * lax.axis_size("ctx")
    f32, bf16 = jnp.float32, jnp.bfloat16
    weight = lax.all_gather(out_weight, "ctx", axis=0, tiled=True)
    kfar, vfar = gather_window(keys, values)
    grad_input = lax.dot_general(
        grad_output, weight, (((1,), (1,)), ((), ())), preferred_element_type=f32
    ).astype(bf16)
    margin = REACH_DEV * rows
    ids = lax.dynamic_slice_in_dim(
        jnp.pad(complex_id, (margin, margin), constant_values=-1), position * rows, rows + 2 * margin
    )
    idk = jnp.broadcast_to(ids[:, None], (rows + 2 * margin, LANES))
    idq = ids[margin : margin + rows].reshape(local_blocks, block)
    local = contacts - (position - REACH_DEV) * local_blocks
    attended, grad_queries, own, far = attention(
        local, contact_count, queries, keys, values, grad_input,
        kfar, vfar, idk, idq,
    )
    grad_keys, grad_values = return_grads(far, own)
    mixed = jnp.dot(attended, weight, preferred_element_type=f32).astype(bf16)
    grad_weight = lax.psum_scatter(
        lax.dot_general(attended, grad_output, (((0,), (0,)), ((), ())), preferred_element_type=f32),
        "ctx",
        scatter_dimension=0,
        tiled=True,
    ) * jnp.float32(1.0 / math.sqrt(total_tokens))
    return mixed, grad_queries, grad_keys, grad_values, grad_weight


def solution(mesh):
    split = P(("groups", "ctx"), None)
    return jax.shard_map(
        shards,
        mesh=mesh,
        in_specs=(split, split, split, P("ctx", None), split, P("groups"), split, P(("groups", "ctx"))),
        out_specs=(split,) * 5,
        check_vma=False,
    )
```

```python
import functools
import math

import jax
import jax.numpy as jnp
from jax import lax
from jax.experimental import pallas as pl
from jax.experimental.pallas import tpu as pltpu
from jax.sharding import PartitionSpec as P

HEADS = 16
REACH_DEV = 2
LANES = 128


def neighbours(n):
    me = lax.axis_index("ctx")
    core, y = lax.rem(me, 2), lax.rem(me // 2, 2)
    ahead, behind = me + 4 - 8 * y, me - 4 + 8 * y
    has_ahead = (ahead >= 0) & (ahead < n)
    has_behind = (behind >= 0) & (behind < n)
    return core, y, me + 2 - 4 * y, me + 1 - 2 * core, ahead, behind, has_ahead, has_behind


def greet(ypeer, cpeer, ahead, behind, has_ahead, has_behind):
    barrier = pltpu.get_barrier_semaphore()

    def hello(device):
        pl.semaphore_signal(barrier, inc=1, device_id={"ctx": device}, device_id_type=pl.DeviceIdType.MESH)

    hello(ypeer)
    hello(cpeer)
    pl.when(has_ahead)(lambda: hello(ahead))
    pl.when(has_behind)(lambda: hello(behind))
    pl.semaphore_wait(barrier, 2 + has_ahead.astype(jnp.int32) + has_behind.astype(jnp.int32))


def remote(src, dst, send, recv, device):
    return pltpu.make_async_remote_copy(
        src_ref=src, dst_ref=dst, send_sem=send, recv_sem=recv,
        device_id={"ctx": device}, device_id_type=pl.DeviceIdType.MESH,
    )


def gather_kernel(n, chunks, k_ref, v_ref, kwin, vwin, sends, recvs):
    core, y, ypeer, cpeer, ahead, behind, has_ahead, has_behind = neighbours(n)
    greet(ypeer, cpeer, ahead, behind, has_ahead, has_behind)
    step = k_ref.shape[0] // chunks
    owns, wins = (k_ref, v_ref), (kwin, vwin)
    total = 2 * chunks

    def at(c):
        return c % 2, pl.ds((c // 2) * step, step)

    def over_y(c):
        a, r = at(c)
        return remote(owns[a].at[r], wins[a].at[3 * y, r], sends.at[0, c], recvs.at[0, c], ypeer)

    def over_z(c):
        a, r = at(c)
        return remote(wins[a].at[3 - 3 * y, r], wins[a].at[3 * y, r], sends.at[1, c], recvs.at[1, c], ahead)

    def across(c):
        a, r = at(c)
        return remote(owns[a].at[r], wins[a].at[1 + core, r], sends.at[2, c], recvs.at[2, c], cpeer)

    def onward(c):
        a, r = at(c)
        return remote(
            wins[a].at[3 - 3 * core, r], wins[a].at[2 - core, r], sends.at[3, c], recvs.at[3, c], cpeer
        )

    def late(c):
        pl.when(has_behind)(lambda: over_z(c).wait_recv())
        pl.when(has_behind & (y != core))(lambda: onward(c).start())

    for c in range(total):
        over_y(c).start()
    for c in range(total):
        across(c).start()
    for c in range(total):
        over_y(c).wait_recv()
        pl.when(has_ahead)(lambda c=c: over_z(c).start())
        pl.when(y == core)(lambda c=c: onward(c).start())
        if c:
            late(c - 1)
    late(total - 1)
    for c in range(total):
        over_y(c).wait_send()
        pl.when(has_ahead)(lambda c=c: over_z(c).wait_send())
        across(c).wait_send()
        across(c).wait_recv()
        pl.when((y == core) | has_behind)(lambda c=c: onward(c).wait_send())
        pl.when((y != core) | has_behind)(lambda c=c: onward(c).wait_recv())


def gather_window(keys, values, chunks=6):
    n = lax.axis_size("ctx")
    any_space = pl.BlockSpec(memory_space=pl.ANY)
    shape = jax.ShapeDtypeStruct((2 * REACH_DEV,) + keys.shape, keys.dtype)
    return pl.pallas_call(
        functools.partial(gather_kernel, n, chunks),
        out_shape=[shape, shape],
        in_specs=[any_space] * 2,
        out_specs=[any_space] * 2,
        scratch_shapes=[pltpu.SemaphoreType.DMA((4, 2 * chunks)), pltpu.SemaphoreType.DMA((4, 2 * chunks))],
        compiler_params=pltpu.CompilerParams(collective_id=0, has_side_effects=True),
        cost_estimate=pl.CostEstimate(flops=0, bytes_accessed=150_000_000, transcendentals=0),
        name="gather_window",
    )(keys, values)


def return_kernel(n, chunks, far, own, gk_ref, gv_ref, got_f, got_c, got_z, got_y, put_z, put_y, sends, recvs):
    core, y, ypeer, cpeer, ahead, behind, has_ahead, has_behind = neighbours(n)
    greet(ypeer, cpeer, ahead, behind, has_ahead, has_behind)
    step = own.shape[1] // chunks
    total = 2 * chunks
    f32, bf16 = jnp.float32, jnp.bfloat16

    def at(c):
        return c % 2, pl.ds((c // 2) * step, step)

    def back(c):
        a, r = at(c)
        return remote(far.at[1 + core, a, r], got_f.at[a, r], sends.at[0, c], recvs.at[0, c], cpeer)

    def across(c):
        a, r = at(c)
        return remote(far.at[2 - core, a, r], got_c.at[a, r], sends.at[1, c], recvs.at[1, c], cpeer)

    def over_z(c):
        a, r = at(c)
        return remote(put_z.at[a, r], got_z.at[a, r], sends.at[2, c], recvs.at[2, c], behind)

    def over_y(c):
        a, r = at(c)
        return remote(put_y.at[a, r], got_y.at[a, r], sends.at[3, c], recvs.at[3, c], ypeer)

    sent_back = (y != core) | has_behind
    got_back = (y == core) | has_behind
    for c in range(total):
        pl.when(sent_back)(lambda c=c: back(c).start())

    def second(c):
        a, r = at(c)
        pl.when(has_ahead)(lambda: over_z(c).wait_recv())
        value = far[3 - 3 * y, a, r, :].astype(f32)
        value = value + jnp.where(has_ahead, got_z[a, r, :].astype(f32), 0.0)
        value = value + jnp.where(y == core, got_f[a, r, :].astype(f32), 0.0)
        put_y[a, r, :] = value.astype(bf16)
        over_y(c).start()

    for c in range(total):
        a, r = at(c)
        pl.when(got_back)(lambda c=c: back(c).wait_recv())
        value = far[3 * y, a, r, :].astype(f32)
        put_z[a, r, :] = (value + jnp.where(y != core, got_f[a, r, :].astype(f32), 0.0)).astype(bf16)
        pl.when(has_behind)(lambda c=c: over_z(c).start())
        across(c).start()
        if c >= 2:
            second(c - 2)
    second(total - 2)
    second(total - 1)
    for c in range(total):
        a, r = at(c)
        across(c).wait_recv()
        over_y(c).wait_recv()
        value = own[a, r, :] + got_c[a, r, :].astype(f32) + got_y[a, r, :].astype(f32)
        (gk_ref, gv_ref)[a][r, :] = value.astype(bf16)
    for c in range(total):
        pl.when(sent_back)(lambda c=c: back(c).wait_send())
        across(c).wait_send()
        pl.when(has_behind)(lambda c=c: over_z(c).wait_send())
        over_y(c).wait_send()


def return_grads(far, own, chunks=6):
    n = lax.axis_size("ctx")
    _, rows, width = own.shape
    space = pl.BlockSpec(memory_space=pltpu.VMEM)
    shape = jax.ShapeDtypeStruct((rows, width), jnp.bfloat16)
    return pl.pallas_call(
        functools.partial(return_kernel, n, chunks),
        out_shape=[shape, shape],
        in_specs=[space] * 2,
        out_specs=[space] * 2,
        scratch_shapes=[pltpu.VMEM((2, rows, width), jnp.bfloat16)] * 6
        + [pltpu.SemaphoreType.DMA((4, 2 * chunks)), pltpu.SemaphoreType.DMA((4, 2 * chunks))],
        compiler_params=pltpu.CompilerParams(
            collective_id=1, has_side_effects=True, vmem_limit_bytes=56 * 1024 * 1024
        ),
        cost_estimate=pl.CostEstimate(flops=0, bytes_accessed=150_000_000, transcendentals=0),
        name="return_grads",
    )(far, own)


def attention_kernel(
    blocks, listed, block, head_dim,
    local_ref, count_ref, q_ref, k_ref, v_ref, d_ref,
    kfar, vfar, idk_ref, idq_ref,
    att_ref, dq_ref, own_ref, far_ref,
    kwin, vwin, bias, gk, gv, kg, vg,
):
    rows = blocks * block
    scale = 1.0 / math.sqrt(head_dim)
    f32, bf16 = jnp.float32, jnp.bfloat16

    @pl.when(pl.program_id(0) == 0)
    def _():
        for b in range(blocks):
            mine = idq_ref[b : b + 1, :]
            for j in range(listed):
                start = pl.multiple_of(local_ref[b, j] * block, block)
                same = idk_ref[pl.ds(start, block), :] == mine
                alive = jnp.where(j < count_ref[b], 0.0, -jnp.inf).astype(f32)
                bias[pl.ds((b * listed + j) * block, block), :] = jnp.where(same, alive, -jnp.inf)

    for i, piece in enumerate((0, 1, None, 2, 3)):
        span = pl.ds(i * rows, rows)
        kwin[span, :] = k_ref[...] if piece is None else kfar[piece]
        vwin[span, :] = v_ref[...] if piece is None else vfar[piece]
    gk[...] = jnp.zeros_like(gk)
    gv[...] = jnp.zeros_like(gv)

    lane = lax.broadcasted_iota(jnp.int32, (block, LANES), 1) < head_dim
    sub = lax.broadcasted_iota(jnp.int32, (LANES, block), 0) < head_dim
    last = (((1,), (1,)), ((), ()))
    first = (((0,), (0,)), ((), ()))

    def two(x):
        zero = jnp.zeros_like(x)
        return jnp.concatenate([jnp.where(lane, x, zero), jnp.where(lane, zero, x)], axis=0).astype(bf16)

    for b in range(blocks):
        here = pl.ds(b * block, block)
        starts = [pl.multiple_of(local_ref[b, j] * block, block) for j in range(listed)]
        for j in range(listed):
            kg[pl.ds(j * block, block), :] = kwin[pl.ds(starts[j], block), :]
            vg[pl.ds(j * block, block), :] = vwin[pl.ds(starts[j], block), :]
        grad = d_ref[here, :].astype(f32)
        q2 = two(q_ref[here, :].astype(f32) * scale)
        d2 = two(grad)
        s = lax.dot_general(kg[...], q2, last, preferred_element_type=f32)
        mask = bias[pl.ds(b * listed * block, listed * block), :]
        s = s + jnp.concatenate([mask, mask], axis=1)
        top = jnp.max(s, axis=0, keepdims=True)
        e = jnp.exp(s - top)
        probs = e * (1.0 / jnp.sum(e, axis=0, keepdims=True))
        low = probs.astype(bf16)
        ot = lax.dot_general(vg[...], low, first, preferred_element_type=f32)
        att = jnp.where(sub, ot[:, :block], ot[:, block:]).astype(bf16).astype(f32)
        att_ref[here, :] = att.T.astype(bf16)
        prod = grad.T * att
        row_dot = jnp.concatenate(
            [jnp.sum(prod[:head_dim], axis=0, keepdims=True), jnp.sum(prod[head_dim:], axis=0, keepdims=True)],
            axis=1,
        )
        dp = lax.dot_general(vg[...], d2, last, preferred_element_type=f32)
        ds = (probs * (dp - row_dot)).astype(bf16)
        dqt = lax.dot_general(kg[...], ds, first, preferred_element_type=f32)
        dq = jnp.where(sub, dqt[:, :block], dqt[:, block:]) * scale
        dq_ref[here, :] = dq.T.astype(bf16)
        dk = jnp.dot(ds, q2, preferred_element_type=f32)
        dv = jnp.dot(low, d2, preferred_element_type=f32)
        for j in range(listed):
            part = slice(j * block, (j + 1) * block)
            gk[pl.ds(starts[j], block), :] += dk[part]
            gv[pl.ds(starts[j], block), :] += dv[part]

    own = pl.ds(REACH_DEV * rows, rows)
    own_ref[0] = gk[own, :]
    own_ref[1] = gv[own, :]
    for i, at in enumerate((0, 1, 3, 4)):
        span = pl.ds(at * rows, rows)
        far_ref[i, 0] = gk[span, :].astype(bf16)
        far_ref[i, 1] = gv[span, :].astype(bf16)


def attention(local, count, queries, keys, values, grad_input, kfar, vfar, idk, idq):
    rows, width = queries.shape
    blocks, listed = local.shape
    block = rows // blocks
    head_dim = width // HEADS
    window = (2 * REACH_DEV + 1) * rows
    flat = pl.BlockSpec((rows, LANES), lambda p, *_: (0, p))
    pair = pl.BlockSpec((2, rows, LANES), lambda p, *_: (0, 0, p))
    quad = pl.BlockSpec((2 * REACH_DEV, rows, LANES), lambda p, *_: (0, 0, p))
    far = pl.BlockSpec((2 * REACH_DEV, 2, rows, LANES), lambda p, *_: (0, 0, 0, p))
    whole = lambda shape: pl.BlockSpec(shape, lambda p, *_: (0, 0))
    f32, bf16 = jnp.float32, jnp.bfloat16
    return pl.pallas_call(
        functools.partial(attention_kernel, blocks, listed, block, head_dim),
        grid_spec=pltpu.PrefetchScalarGridSpec(
            num_scalar_prefetch=2,
            grid=(width // LANES,),
            in_specs=[flat, flat, flat, flat, quad, quad, whole(idk.shape), whole(idq.shape)],
            out_specs=[flat, flat, pair, far],
            scratch_shapes=[
                pltpu.VMEM((window, LANES), bf16),
                pltpu.VMEM((window, LANES), bf16),
                pltpu.VMEM((blocks * listed * block, LANES), f32),
                pltpu.VMEM((window, LANES), f32),
                pltpu.VMEM((window, LANES), f32),
                pltpu.VMEM((listed * block, LANES), bf16),
                pltpu.VMEM((listed * block, LANES), bf16),
            ],
        ),
        out_shape=[
            jax.ShapeDtypeStruct((rows, width), bf16),
            jax.ShapeDtypeStruct((rows, width), bf16),
            jax.ShapeDtypeStruct((2, rows, width), f32),
            jax.ShapeDtypeStruct((2 * REACH_DEV, 2, rows, width), bf16),
        ],
        compiler_params=pltpu.CompilerParams(dimension_semantics=("arbitrary",)),
        name="contact_attention",
    )(local, count, queries, keys, values, grad_input, kfar, vfar, idk, idq)


def shards(queries, keys, values, out_weight, grad_output, complex_id, contacts, contact_count):
    rows, width = queries.shape
    local_blocks, listed = contacts.shape
    block = rows // local_blocks
    position = lax.axis_index("ctx")
    total_tokens = rows * lax.axis_size("ctx")
    f32, bf16 = jnp.float32, jnp.bfloat16
    weight = lax.all_gather(out_weight, "ctx", axis=0, tiled=True)
    kfar, vfar = gather_window(keys, values)
    grad_input = lax.dot_general(
        grad_output, weight, (((1,), (1,)), ((), ())), preferred_element_type=f32
    ).astype(bf16)
    margin = REACH_DEV * rows
    ids = lax.dynamic_slice_in_dim(
        jnp.pad(complex_id, (margin, margin), constant_values=-1), position * rows, rows + 2 * margin
    )
    idk = jnp.broadcast_to(ids[:, None], (rows + 2 * margin, LANES))
    idq = ids[margin : margin + rows].reshape(local_blocks, block)
    local = contacts - (position - REACH_DEV) * local_blocks
    attended, grad_queries, own, far = attention(
        local, contact_count, queries, keys, values, grad_input,
        kfar, vfar, idk, idq,
    )
    grad_keys, grad_values = return_grads(far, own)
    mixed = jnp.dot(attended, weight, preferred_element_type=f32).astype(bf16)
    grad_weight = lax.psum_scatter(
        lax.dot_general(attended, grad_output, (((0,), (0,)), ((), ())), preferred_element_type=f32).astype(bf16),
        "ctx",
        scatter_dimension=0,
        tiled=True,
    ).astype(f32) * jnp.float32(1.0 / math.sqrt(total_tokens))
    return mixed, grad_queries, grad_keys, grad_values, grad_weight


def solution(mesh):
    split = P(("groups", "ctx"), None)
    return jax.shard_map(
        shards,
        mesh=mesh,
        in_specs=(split, split, split, P("ctx", None), split, P("groups"), split, P(("groups", "ctx"))),
        out_specs=(split,) * 5,
        check_vma=False,
    )
```

```python
import functools
import math

import jax
import jax.numpy as jnp
from jax import lax
from jax.experimental import pallas as pl
from jax.experimental.pallas import tpu as pltpu
from jax.sharding import PartitionSpec as P

HEADS = 16
REACH_DEV = 2
LANES = 128


def neighbours(n):
    me = lax.axis_index("ctx")
    core, y = lax.rem(me, 2), lax.rem(me // 2, 2)
    ahead, behind = me + 4 - 8 * y, me - 4 + 8 * y
    has_ahead = (ahead >= 0) & (ahead < n)
    has_behind = (behind >= 0) & (behind < n)
    return core, y, me + 2 - 4 * y, me + 1 - 2 * core, ahead, behind, has_ahead, has_behind


def greet(ypeer, cpeer, ahead, behind, has_ahead, has_behind):
    barrier = pltpu.get_barrier_semaphore()

    def hello(device):
        pl.semaphore_signal(barrier, inc=1, device_id={"ctx": device}, device_id_type=pl.DeviceIdType.MESH)

    hello(ypeer)
    hello(cpeer)
    pl.when(has_ahead)(lambda: hello(ahead))
    pl.when(has_behind)(lambda: hello(behind))
    pl.semaphore_wait(barrier, 2 + has_ahead.astype(jnp.int32) + has_behind.astype(jnp.int32))


def remote(src, dst, send, recv, device):
    return pltpu.make_async_remote_copy(
        src_ref=src, dst_ref=dst, send_sem=send, recv_sem=recv,
        device_id={"ctx": device}, device_id_type=pl.DeviceIdType.MESH,
    )


def gather_kernel(n, chunks, k_ref, v_ref, kwin, vwin, sends, recvs):
    core, y, ypeer, cpeer, ahead, behind, has_ahead, has_behind = neighbours(n)
    greet(ypeer, cpeer, ahead, behind, has_ahead, has_behind)
    step = k_ref.shape[0] // chunks
    owns, wins = (k_ref, v_ref), (kwin, vwin)
    total = 2 * chunks

    def at(c):
        return c % 2, pl.ds((c // 2) * step, step)

    def over_y(c):
        a, r = at(c)
        return remote(owns[a].at[r], wins[a].at[3 * y, r], sends.at[0, c], recvs.at[0, c], ypeer)

    def over_z(c):
        a, r = at(c)
        return remote(wins[a].at[3 - 3 * y, r], wins[a].at[3 * y, r], sends.at[1, c], recvs.at[1, c], ahead)

    def across(c):
        a, r = at(c)
        return remote(owns[a].at[r], wins[a].at[1 + core, r], sends.at[2, c], recvs.at[2, c], cpeer)

    def onward(c):
        a, r = at(c)
        return remote(
            wins[a].at[3 - 3 * core, r], wins[a].at[2 - core, r], sends.at[3, c], recvs.at[3, c], cpeer
        )

    def late(c):
        pl.when(has_behind)(lambda: over_z(c).wait_recv())
        pl.when(has_behind & (y != core))(lambda: onward(c).start())

    for c in range(total):
        over_y(c).start()
    for c in range(total):
        across(c).start()
    for c in range(total):
        over_y(c).wait_recv()
        pl.when(has_ahead)(lambda c=c: over_z(c).start())
        pl.when(y == core)(lambda c=c: onward(c).start())
        if c:
            late(c - 1)
    late(total - 1)
    for c in range(total):
        over_y(c).wait_send()
        pl.when(has_ahead)(lambda c=c: over_z(c).wait_send())
        across(c).wait_send()
        across(c).wait_recv()
        pl.when((y == core) | has_behind)(lambda c=c: onward(c).wait_send())
        pl.when((y != core) | has_behind)(lambda c=c: onward(c).wait_recv())


def gather_window(keys, values, chunks=12):
    n = lax.axis_size("ctx")
    any_space = pl.BlockSpec(memory_space=pl.ANY)
    shape = jax.ShapeDtypeStruct((2 * REACH_DEV,) + keys.shape, keys.dtype)
    return pl.pallas_call(
        functools.partial(gather_kernel, n, chunks),
        out_shape=[shape, shape],
        in_specs=[any_space] * 2,
        out_specs=[any_space] * 2,
        scratch_shapes=[pltpu.SemaphoreType.DMA((4, 2 * chunks)), pltpu.SemaphoreType.DMA((4, 2 * chunks))],
        compiler_params=pltpu.CompilerParams(collective_id=0, has_side_effects=True),
        cost_estimate=pl.CostEstimate(flops=0, bytes_accessed=150_000_000, transcendentals=0),
        name="gather_window",
    )(keys, values)


def return_kernel(n, chunks, far, own, gk_ref, gv_ref, got_f, got_c, got_z, got_y, put_z, put_y, sends, recvs):
    core, y, ypeer, cpeer, ahead, behind, has_ahead, has_behind = neighbours(n)
    greet(ypeer, cpeer, ahead, behind, has_ahead, has_behind)
    step = own.shape[1] // chunks
    total = 2 * chunks
    f32, bf16 = jnp.float32, jnp.bfloat16

    def at(c):
        return c % 2, pl.ds((c // 2) * step, step)

    def back(c):
        a, r = at(c)
        return remote(far.at[1 + core, a, r], got_f.at[a, r], sends.at[0, c], recvs.at[0, c], cpeer)

    def across(c):
        a, r = at(c)
        return remote(far.at[2 - core, a, r], got_c.at[a, r], sends.at[1, c], recvs.at[1, c], cpeer)

    def over_z(c):
        a, r = at(c)
        return remote(put_z.at[a, r], got_z.at[a, r], sends.at[2, c], recvs.at[2, c], behind)

    def over_y(c):
        a, r = at(c)
        return remote(put_y.at[a, r], got_y.at[a, r], sends.at[3, c], recvs.at[3, c], ypeer)

    sent_back = (y != core) | has_behind
    got_back = (y == core) | has_behind
    for c in range(total):
        pl.when(sent_back)(lambda c=c: back(c).start())

    def second(c):
        a, r = at(c)
        pl.when(has_ahead)(lambda: over_z(c).wait_recv())
        value = far[3 - 3 * y, a, r, :].astype(f32)
        value = value + jnp.where(has_ahead, got_z[a, r, :].astype(f32), 0.0)
        value = value + jnp.where(y == core, got_f[a, r, :].astype(f32), 0.0)
        put_y[a, r, :] = value.astype(bf16)
        over_y(c).start()

    for c in range(total):
        a, r = at(c)
        pl.when(got_back)(lambda c=c: back(c).wait_recv())
        value = far[3 * y, a, r, :].astype(f32)
        put_z[a, r, :] = (value + jnp.where(y != core, got_f[a, r, :].astype(f32), 0.0)).astype(bf16)
        pl.when(has_behind)(lambda c=c: over_z(c).start())
        across(c).start()
        if c >= 2:
            second(c - 2)
    second(total - 2)
    second(total - 1)
    for c in range(total):
        a, r = at(c)
        across(c).wait_recv()
        over_y(c).wait_recv()
        value = own[a, r, :] + got_c[a, r, :].astype(f32) + got_y[a, r, :].astype(f32)
        (gk_ref, gv_ref)[a][r, :] = value.astype(bf16)
    for c in range(total):
        pl.when(sent_back)(lambda c=c: back(c).wait_send())
        across(c).wait_send()
        pl.when(has_behind)(lambda c=c: over_z(c).wait_send())
        over_y(c).wait_send()


def return_grads(far, own, chunks=12):
    n = lax.axis_size("ctx")
    _, rows, width = own.shape
    space = pl.BlockSpec(memory_space=pltpu.VMEM)
    shape = jax.ShapeDtypeStruct((rows, width), jnp.bfloat16)
    return pl.pallas_call(
        functools.partial(return_kernel, n, chunks),
        out_shape=[shape, shape],
        in_specs=[space] * 2,
        out_specs=[space] * 2,
        scratch_shapes=[pltpu.VMEM((2, rows, width), jnp.bfloat16)] * 6
        + [pltpu.SemaphoreType.DMA((4, 2 * chunks)), pltpu.SemaphoreType.DMA((4, 2 * chunks))],
        compiler_params=pltpu.CompilerParams(
            collective_id=1, has_side_effects=True, vmem_limit_bytes=56 * 1024 * 1024
        ),
        cost_estimate=pl.CostEstimate(flops=0, bytes_accessed=150_000_000, transcendentals=0),
        name="return_grads",
    )(far, own)


def attention_kernel(
    blocks, listed, block, head_dim,
    local_ref, count_ref, q_ref, k_ref, v_ref, d_ref,
    kfar, vfar, idk_ref, idq_ref,
    att_ref, dq_ref, own_ref, far_ref,
    kwin, vwin, bias, gk, gv, kg, vg,
):
    rows = blocks * block
    scale = 1.0 / math.sqrt(head_dim)
    f32, bf16 = jnp.float32, jnp.bfloat16

    @pl.when(pl.program_id(0) == 0)
    def _():
        for b in range(blocks):
            mine = idq_ref[b : b + 1, :]
            for j in range(listed):
                start = pl.multiple_of(local_ref[b, j] * block, block)
                same = idk_ref[pl.ds(start, block), :] == mine
                alive = jnp.where(j < count_ref[b], 0.0, -jnp.inf).astype(f32)
                bias[pl.ds((b * listed + j) * block, block), :] = jnp.where(same, alive, -jnp.inf)

    for i, piece in enumerate((0, 1, None, 2, 3)):
        span = pl.ds(i * rows, rows)
        kwin[span, :] = k_ref[...] if piece is None else kfar[piece]
        vwin[span, :] = v_ref[...] if piece is None else vfar[piece]
    gk[...] = jnp.zeros_like(gk)
    gv[...] = jnp.zeros_like(gv)

    lane = lax.broadcasted_iota(jnp.int32, (block, LANES), 1) < head_dim
    sub = lax.broadcasted_iota(jnp.int32, (LANES, block), 0) < head_dim
    last = (((1,), (1,)), ((), ()))
    first = (((0,), (0,)), ((), ()))

    def two(x):
        zero = jnp.zeros_like(x)
        return jnp.concatenate([jnp.where(lane, x, zero), jnp.where(lane, zero, x)], axis=0).astype(bf16)

    for b in range(blocks):
        here = pl.ds(b * block, block)
        starts = [pl.multiple_of(local_ref[b, j] * block, block) for j in range(listed)]
        for j in range(listed):
            kg[pl.ds(j * block, block), :] = kwin[pl.ds(starts[j], block), :]
            vg[pl.ds(j * block, block), :] = vwin[pl.ds(starts[j], block), :]
        grad = d_ref[here, :].astype(f32)
        q2 = two(q_ref[here, :].astype(f32) * scale)
        d2 = two(grad)
        s = lax.dot_general(kg[...], q2, last, preferred_element_type=f32)
        mask = bias[pl.ds(b * listed * block, listed * block), :]
        s = s + jnp.concatenate([mask, mask], axis=1)
        top = jnp.max(s, axis=0, keepdims=True)
        e = jnp.exp(s - top)
        probs = e * (1.0 / jnp.sum(e, axis=0, keepdims=True))
        low = probs.astype(bf16)
        ot = lax.dot_general(vg[...], low, first, preferred_element_type=f32)
        att = jnp.where(sub, ot[:, :block], ot[:, block:]).astype(bf16).astype(f32)
        att_ref[here, :] = att.T.astype(bf16)
        prod = grad.T * att
        row_dot = jnp.concatenate(
            [jnp.sum(prod[:head_dim], axis=0, keepdims=True), jnp.sum(prod[head_dim:], axis=0, keepdims=True)],
            axis=1,
        )
        dp = lax.dot_general(vg[...], d2, last, preferred_element_type=f32)
        ds = (probs * (dp - row_dot)).astype(bf16)
        dqt = lax.dot_general(kg[...], ds, first, preferred_element_type=f32)
        dq = jnp.where(sub, dqt[:, :block], dqt[:, block:]) * scale
        dq_ref[here, :] = dq.T.astype(bf16)
        dk = jnp.dot(ds, q2, preferred_element_type=f32)
        dv = jnp.dot(low, d2, preferred_element_type=f32)
        for j in range(listed):
            part = slice(j * block, (j + 1) * block)
            gk[pl.ds(starts[j], block), :] += dk[part]
            gv[pl.ds(starts[j], block), :] += dv[part]

    own = pl.ds(REACH_DEV * rows, rows)
    own_ref[0] = gk[own, :]
    own_ref[1] = gv[own, :]
    for i, at in enumerate((0, 1, 3, 4)):
        span = pl.ds(at * rows, rows)
        far_ref[i, 0] = gk[span, :].astype(bf16)
        far_ref[i, 1] = gv[span, :].astype(bf16)


def attention(local, count, queries, keys, values, grad_input, kfar, vfar, idk, idq):
    rows, width = queries.shape
    blocks, listed = local.shape
    block = rows // blocks
    head_dim = width // HEADS
    window = (2 * REACH_DEV + 1) * rows
    flat = pl.BlockSpec((rows, LANES), lambda p, *_: (0, p))
    pair = pl.BlockSpec((2, rows, LANES), lambda p, *_: (0, 0, p))
    quad = pl.BlockSpec((2 * REACH_DEV, rows, LANES), lambda p, *_: (0, 0, p))
    far = pl.BlockSpec((2 * REACH_DEV, 2, rows, LANES), lambda p, *_: (0, 0, 0, p))
    whole = lambda shape: pl.BlockSpec(shape, lambda p, *_: (0, 0))
    f32, bf16 = jnp.float32, jnp.bfloat16
    return pl.pallas_call(
        functools.partial(attention_kernel, blocks, listed, block, head_dim),
        grid_spec=pltpu.PrefetchScalarGridSpec(
            num_scalar_prefetch=2,
            grid=(width // LANES,),
            in_specs=[flat, flat, flat, flat, quad, quad, whole(idk.shape), whole(idq.shape)],
            out_specs=[flat, flat, pair, far],
            scratch_shapes=[
                pltpu.VMEM((window, LANES), bf16),
                pltpu.VMEM((window, LANES), bf16),
                pltpu.VMEM((blocks * listed * block, LANES), f32),
                pltpu.VMEM((window, LANES), f32),
                pltpu.VMEM((window, LANES), f32),
                pltpu.VMEM((listed * block, LANES), bf16),
                pltpu.VMEM((listed * block, LANES), bf16),
            ],
        ),
        out_shape=[
            jax.ShapeDtypeStruct((rows, width), bf16),
            jax.ShapeDtypeStruct((rows, width), bf16),
            jax.ShapeDtypeStruct((2, rows, width), f32),
            jax.ShapeDtypeStruct((2 * REACH_DEV, 2, rows, width), bf16),
        ],
        compiler_params=pltpu.CompilerParams(dimension_semantics=("arbitrary",)),
        name="contact_attention",
    )(local, count, queries, keys, values, grad_input, kfar, vfar, idk, idq)


def shards(queries, keys, values, out_weight, grad_output, complex_id, contacts, contact_count):
    rows, width = queries.shape
    local_blocks, listed = contacts.shape
    block = rows // local_blocks
    position = lax.axis_index("ctx")
    total_tokens = rows * lax.axis_size("ctx")
    f32, bf16 = jnp.float32, jnp.bfloat16
    weight = lax.all_gather(out_weight, "ctx", axis=0, tiled=True)
    kfar, vfar = gather_window(keys, values)
    grad_input = lax.dot_general(
        grad_output, weight, (((1,), (1,)), ((), ())), preferred_element_type=f32
    ).astype(bf16)
    margin = REACH_DEV * rows
    ids = lax.dynamic_slice_in_dim(
        jnp.pad(complex_id, (margin, margin), constant_values=-1), position * rows, rows + 2 * margin
    )
    idk = jnp.broadcast_to(ids[:, None], (rows + 2 * margin, LANES))
    idq = ids[margin : margin + rows].reshape(local_blocks, block)
    local = contacts - (position - REACH_DEV) * local_blocks
    attended, grad_queries, own, far = attention(
        local, contact_count, queries, keys, values, grad_input,
        kfar, vfar, idk, idq,
    )
    grad_keys, grad_values = return_grads(far, own)
    mixed = jnp.dot(attended, weight, preferred_element_type=f32).astype(bf16)
    grad_weight = lax.psum_scatter(
        lax.dot_general(attended, grad_output, (((0,), (0,)), ((), ())), preferred_element_type=f32).astype(bf16),
        "ctx",
        scatter_dimension=0,
        tiled=True,
    ).astype(f32) * jnp.float32(1.0 / math.sqrt(total_tokens))
    return mixed, grad_queries, grad_keys, grad_values, grad_weight


def solution(mesh):
    split = P(("groups", "ctx"), None)
    return jax.shard_map(
        shards,
        mesh=mesh,
        in_specs=(split, split, split, P("ctx", None), split, P("groups"), split, P(("groups", "ctx"))),
        out_specs=(split,) * 5,
        check_vma=False,
    )
```
